256 devices in a mesh: gz: 16 (over z, y_hi), xy: 16 (over x, y_lo, core).
Axes of the slice: x: 4, y: 4 (y_hi: 2, y_lo: 2; y = y_hi * 2 + y_lo), z: 8, core: 2. Of those that a mesh axis runs over, the one named last changes fastest.
Arguments:
- view_one: float32 [256, 1024, 256], P('gz', 'xy'), may hold values from 0.2 to 5
- view_two: float32 [256, 1024, 256], P('gz', 'xy'), may hold values from 0.2 to 5
- estimate: float32 [256, 1024, 256], P('gz', 'xy'), may hold values from 0.5 to 2
- psf: float32 [2, 3, 15], replicated, may hold values from 0.05 to 1
Outputs:
- updated: float32 [256, 1024, 256], P('gz', 'xy')
The draws below stay inside these ranges and needn't reach their ends.
All inputs are finite; a program needn't handle non-finite values.
Results may differ from the reference program's by a relative error of at most 0.00005.
Values sent between devices are 32-bit elements; how exact they have to be, the bound alone decides.
No kernel may reach another device: no remote copies, remote signals or barrier semaphores. Data moves between devices by JAX's collectives and lax.ppermute only.
A program may use at most 64 MiB of HBM per device.

```python
import math
import jax
import jax.numpy as jnp

CX = 256
TAPS = 15
ITERS = 2
NZ = 256
NY = 1024


def levels(key, shape, split, least, top_value):
    factor_of, own = 1.0, jax.random.fold_in(key, 6)
    for position, parts in split:
        steps = jnp.exp(jax.random.uniform(jax.random.fold_in(own, position), (parts,), jnp.float32, least / len(split), top_value / len(split)))
        factor_of = factor_of * jnp.repeat(steps, shape[position] // parts).reshape([-1 if axis == position else 1 for axis in range(len(shape))])
    return factor_of


def setup_inputs(seed: int = 0) -> dict:
    seeds = jax.random.split(jax.random.key(seed), 5)
    view_one = jnp.clip(jnp.exp(math.log(5.0) - 3.218876 * jax.random.uniform(seeds[0], (NZ, NY, CX), jnp.float32) ** levels(seeds[0], (NZ, NY, CX), ((0, 16), (1, 16)), -0.2, 0.2)), 0.2, 5.0)
    view_two = jnp.clip(jnp.exp(math.log(5.0) - 3.218876 * jax.random.uniform(seeds[1], (NZ, NY, CX), jnp.float32) ** levels(seeds[1], (NZ, NY, CX), ((0, 16), (1, 16)), -0.2, 0.2)), 0.2, 5.0)
    estimate = jnp.clip(jnp.exp(math.log(2.0) - 1.3862944 * jax.random.uniform(seeds[2], (NZ, NY, CX), jnp.float32) ** levels(seeds[2], (NZ, NY, CX), ((0, 16), (1, 16)), -0.2, 0.2)), 0.5, 2.0)
    psf = jnp.clip(jnp.exp(jax.random.uniform(seeds[3], (2, 3, TAPS), jnp.float32, math.log(0.05), math.log(1.0))), 0.05, 1.0)
    return dict(view_one=view_one, view_two=view_two, estimate=estimate, psf=psf)


def taps_along(padded, weights, dim, length):
    total = weights[0] * jax.lax.slice_in_dim(padded, 0, length, axis=dim)
    for tap_index in range(1, weights.shape[0]):
        total = total + weights[tap_index] * jax.lax.slice_in_dim(padded, tap_index, tap_index + length, axis=dim)
    return total


def apply_blur(field, kernels):
    half = kernels.shape[1] // 2
    depth, rows, width = field.shape
    along_z = taps_along(jnp.pad(field, ((half, half), (0, 0), (0, 0))), kernels[0], 0, depth)
    along_y = taps_along(jnp.pad(along_z, ((0, 0), (half, half), (0, 0))), kernels[1], 1, rows)
    return taps_along(jnp.pad(along_y, ((0, 0), (0, 0), (half, half))), kernels[2], 2, width)


def reference(view_one, view_two, estimate, psf):
    kernels = psf / jnp.sum(psf, axis=2, keepdims=True)
    forward_one = kernels[0]
    adjoint_one = kernels[0][:, ::-1]
    forward_two = kernels[1]
    adjoint_two = kernels[1][:, ::-1]
    for step_index in range(ITERS):
        back_one = apply_blur(view_one / apply_blur(estimate, forward_one), adjoint_one)
        blurred_two = apply_blur(estimate[::-1], forward_two)
        back_two = apply_blur(view_two / blurred_two, adjoint_two)[::-1]
        estimate = estimate * (back_one + back_two) * 0.5
    return estimate
```

```python
import functools

import jax
import jax.numpy as jnp
from jax import lax
from jax.experimental import pallas as pl
from jax.experimental.pallas import tpu as pltpu
from jax.sharding import PartitionSpec as P

EDGE = 8
CHUNK = 4
F32 = jnp.float32
BF16 = jnp.bfloat16


def moved(value, axis, target):
    count = lax.axis_size(axis)
    pairs = [(i, target(i)) for i in range(count) if 0 <= target(i) < count]
    return lax.ppermute(value, axis, pairs)


def split(value):
    high = value.astype(BF16)
    low = (value - high.astype(F32)).astype(BF16)
    return high, low


def split_outside(value):
    high = lax.reduce_precision(value, 8, 7)
    return high.astype(BF16), (value - high).astype(BF16)


def band(weights, rows, columns, shift):
    offsets = jnp.arange(rows)[:, None] - jnp.arange(columns)[None, :] + shift
    matrix = jnp.zeros((rows, columns), F32)
    for tap in range(weights.shape[0]):
        matrix = matrix + jnp.where(offsets == tap, weights[tap], 0.0)
    return matrix


def filters(kernels, rows, width):
    taps = kernels.shape[1]
    half = taps // 2
    forward = band(kernels[1], rows + 2 * EDGE, rows, half - EDGE).T
    lefts = []
    for matrix in (forward, forward.T):
        high, low = split_outside(matrix)
        lefts.append(jnp.concatenate([high, high, low], axis=1))
    across = band(kernels[2], width, width, half)
    rights = []
    for matrix in (across, across.T):
        high, low = split_outside(matrix)
        rights.append(jnp.stack([high, low]))
    return kernels[0], lefts[0], lefts[1], rights[0], rights[1]


def gather_planes(taps, planes, depth):
    outs = []
    for z in range(depth):
        total = taps[0] * planes[z]
        for t in range(1, len(taps)):
            total = total + taps[t] * planes[z + t]
        outs.append(total)
    return outs


def scatter_planes(tap_lists, plane_lists):
    depth = len(plane_lists[0])
    count = len(tap_lists[0])
    outs = []
    for o in range(depth + count - 1):
        total = None
        for taps, planes in zip(tap_lists, plane_lists):
            for z in range(max(0, o - count + 1), min(depth, o + 1)):
                term = taps[o - z] * planes[z]
                total = term if total is None else total + term
        outs.append(total)
    return outs


def z_forward(taps, field, out_ref):
    center, z_low, z_high, y_low, y_high = field
    depth, rows, width = center.shape
    reach = z_low.shape[0]

    def strip(first_row, planes_of):
        for lane in range(0, width, 128):
            lanes = pl.ds(lane, 128)
            planes = planes_of(lanes)
            for z, total in enumerate(gather_planes(taps, planes, depth)):
                out_ref[z, pl.ds(first_row, EDGE), lanes] = total

    def inner(step, carry):
        row = pl.multiple_of(step * EDGE, EDGE)

        def planes_of(lanes):
            window = pl.ds(row, EDGE)
            return (
                [z_low[z, window, lanes] for z in range(reach)]
                + [center[z, window, lanes] for z in range(depth)]
                + [z_high[z, window, lanes] for z in range(reach)]
            )

        strip(row + EDGE, planes_of)
        return carry

    lax.fori_loop(0, rows // EDGE, inner, 0)
    strip(0, lambda lanes: [y_low[z, :, lanes] for z in range(depth + 2 * reach)])
    strip(rows + EDGE, lambda lanes: [y_high[z, :, lanes] for z in range(depth + 2 * reach)])


def left_product(matrix, value):
    high, low = split(value)
    stacked = jnp.concatenate([high, low, high], axis=0)
    return jnp.dot(matrix, stacked, preferred_element_type=F32)


def right_product(value, matrix_ref):
    high, low = split(value)
    dot = functools.partial(jnp.dot, preferred_element_type=F32)
    return dot(high, matrix_ref[0]) + dot(low, matrix_ref[0]) + dot(high, matrix_ref[1])


def blurred_chunk(along_z, first, left, right):
    rows = [left_product(left[...], along_z[first + k]) for k in range(CHUNK)]
    return right_product(jnp.concatenate(rows, axis=0), right)


def back_chunk(ratio, first, left, right, out_ref):
    rows = out_ref.shape[1] - 2 * EDGE
    across = right_product(ratio, right)
    for k in range(CHUNK):
        out_ref[first + k] = left_product(left[...], across[k * rows : (k + 1) * rows])


def z_back(tap_lists, sources, outs, extra):
    center, y_low, y_high = outs
    depth = sources[0].shape[0]
    rows, width = center.shape[1:]

    def strip(source_row, out_ref, extra_ref, out_row):
        for lane in range(0, width, 128):
            lanes = pl.ds(lane, 128)
            plane_lists = [
                [ref[z, pl.ds(source_row, EDGE), lanes] for z in range(depth)] for ref in sources
            ]
            for o, total in enumerate(scatter_planes(tap_lists, plane_lists)):
                if extra_ref is not None:
                    total = total + extra_ref[o, pl.ds(out_row, EDGE), lanes]
                out_ref[o, pl.ds(out_row, EDGE), lanes] = total

    def inner(step, carry):
        row = pl.multiple_of(step * EDGE, EDGE)
        strip(row + EDGE, center, extra and extra[0], row)
        return carry

    lax.fori_loop(0, rows // EDGE, inner, 0)
    strip(0, y_low, extra and extra[1], 0)
    strip(rows + EDGE, y_high, extra and extra[2], 0)


def read_taps(ref, view, flip):
    taps = [ref[view, t] for t in range(ref.shape[1])]
    return taps[::-1] if flip else taps


def first_kernel(taps_ref, *refs):
    field, refs = refs[:5], refs[5:]
    view_one = refs[0]
    left_one, back_left_one, right_one, back_right_one, left_two, right_two = refs[1:7]
    partial, blurred_two = refs[7:10], refs[10]
    along_z, back = refs[11:13]
    depth, rows, _ = view_one.shape
    one, two = read_taps(taps_ref, 0, False), read_taps(taps_ref, 1, True)
    z_forward(one, field, along_z)
    for first in range(0, depth, CHUNK):
        blurred = blurred_chunk(along_z, first, left_one, right_one)
        seen = jnp.concatenate([view_one[first + k] for k in range(CHUNK)], axis=0)
        back_chunk(seen / blurred, first, back_left_one, back_right_one, back)
    z_back([one], [back], partial, None)
    z_forward(two, field, along_z)
    for first in range(0, depth, CHUNK):
        blurred = blurred_chunk(along_z, first, left_two, right_two)
        for k in range(CHUNK):
            blurred_two[first + k] = blurred[k * rows : (k + 1) * rows]


def second_kernel(taps_ref, blurred_two, view_two, back_left, back_right, *refs):
    extra, outs, back = refs[:3], refs[3:6], refs[6]
    depth = view_two.shape[0]
    for first in range(0, depth, CHUNK):
        ratio = jnp.concatenate(
            [view_two[depth - 1 - first - k] / blurred_two[first + k] for k in range(CHUNK)],
            axis=0,
        )
        back_chunk(ratio, first, back_left, back_right, back)
    z_back([read_taps(taps_ref, 1, True)], [back], outs, extra)


def both_kernel(taps_ref, *refs):
    field, refs = refs[:5], refs[5:]
    views, refs = refs[:2], refs[2:]
    matrices = (refs[:4], refs[4:8])
    outs, along_z, backs = refs[8:11], refs[11], refs[12:14]
    depth = views[0].shape[0]
    taps = [read_taps(taps_ref, 0, False), read_taps(taps_ref, 1, True)]
    for v in range(2):
        left, back_left, right, back_right = matrices[v]
        z_forward(taps[v], field, along_z)
        for first in range(0, depth, CHUNK):
            blurred = blurred_chunk(along_z, first, left, right)
            planes = [first + k if v == 0 else depth - 1 - first - k for k in range(CHUNK)]
            seen = jnp.concatenate([views[v][z] for z in planes], axis=0)
            back_chunk(seen / blurred, first, back_left, back_right, backs[v])
    z_back(taps, backs, outs, None)


def call(kernel, arrays, outs, scratch):
    vmem = pl.BlockSpec(memory_space=pltpu.VMEM)
    return pl.pallas_call(
        kernel,
        out_shape=[jax.ShapeDtypeStruct(shape, F32) for shape in outs],
        in_specs=[pl.BlockSpec(memory_space=pltpu.SMEM)] + [vmem] * (len(arrays) - 1),
        out_specs=[vmem] * len(outs),
        scratch_shapes=[pltpu.VMEM(shape, F32) for shape in scratch],
    )(*arrays)


def row_halos(center, z_low, z_high):
    def rows(window):
        return jnp.concatenate([z_low[:, window], center[:, window], z_high[:, window]], axis=0)

    low = moved(rows(slice(-EDGE, None)), "xy", lambda i: i + 1)
    high = moved(rows(slice(None, EDGE)), "xy", lambda i: i - 1)
    return low, high


def rows_added(partial):
    center, low, high = partial
    from_below = moved(high, "xy", lambda i: i + 1)
    from_above = moved(low, "xy", lambda i: i - 1)
    rows = center.shape[1]
    return jnp.concatenate(
        [
            center[:, :EDGE] + from_below,
            center[:, EDGE : rows - EDGE],
            center[:, rows - EDGE :] + from_above,
        ],
        axis=1,
    )


def local(view_one, view_two, estimate, psf):
    depth, rows, width = estimate.shape
    kernels = psf / jnp.sum(psf, axis=2, keepdims=True)
    reach = psf.shape[2] // 2
    z_taps = kernels[:, 0]
    one = filters(kernels[0], rows, width)[1:]
    two = filters(kernels[1], rows, width)[1:]

    z_low = moved(estimate[depth - reach :], "gz", lambda i: i + 1)
    z_high = moved(estimate[:reach], "gz", lambda i: i - 1)
    count = lax.axis_size("gz")
    view_two = moved(view_two, "gz", lambda i: count - 1 - i)

    full = depth + 2 * reach
    partial_shapes = [(full, rows, width), (full, EDGE, width), (full, EDGE, width)]
    tall = (depth, rows + 2 * EDGE, width)

    y_low, y_high = row_halos(estimate, z_low, z_high)
    field = (estimate, z_low, z_high, y_low, y_high)
    *partial, blurred_two = call(
        first_kernel,
        (z_taps, *field, view_one, *one, two[0], two[2]),
        partial_shapes + [view_one.shape],
        [tall, tall],
    )
    partial = call(
        second_kernel,
        (z_taps, blurred_two, view_two, two[1], two[3], *partial),
        partial_shapes,
        [tall],
    )
    total = rows_added(partial)
    overlap = 2 * reach
    below = total[:overlap] + moved(total[full - overlap :], "gz", lambda i: i + 1)
    above = total[full - overlap :] + moved(total[:overlap], "gz", lambda i: i - 1)
    z_low = z_low * below[:reach] * 0.5
    z_high = z_high * above[reach:] * 0.5
    estimate = (
        estimate
        * jnp.concatenate([below[reach:], total[overlap : full - overlap], above[:reach]], axis=0)
        * 0.5
    )

    y_low, y_high = row_halos(estimate, z_low, z_high)
    field = (estimate, z_low, z_high, y_low, y_high)
    partial = call(
        both_kernel,
        (z_taps, *field, view_one, view_two, *one, *two),
        partial_shapes,
        [tall, tall, tall],
    )
    total = rows_added(partial)
    from_below = moved(total[full - reach :], "gz", lambda i: i + 1)
    from_above = moved(total[:reach], "gz", lambda i: i - 1)
    center = total[reach : full - reach]
    center = jnp.concatenate(
        [
            center[:reach] + from_below,
            center[reach : depth - reach],
            center[depth - reach :] + from_above,
        ],
        axis=0,
    )
    return estimate * center * 0.5


def solution(mesh):
    return jax.shard_map(
        local,
        mesh=mesh,
        in_specs=(P("gz", "xy", None), P("gz", "xy", None), P("gz", "xy", None), P()),
        out_specs=P("gz", "xy", None),
        check_vma=False,
    )
```

```python
import functools

import jax
import jax.numpy as jnp
from jax import lax
from jax.experimental import pallas as pl
from jax.experimental.pallas import tpu as pltpu
from jax.sharding import PartitionSpec as P

EDGE = 8
CHUNK = 4
F32 = jnp.float32
BF16 = jnp.bfloat16


AXES = ("gz", "xy")
SLABS = 16
TILES = 16


def given(slab, tile):
    return slab * TILES + tile


def working(slab, tile):
    return given(slab - slab % 2 + tile % 2, tile - tile % 2 + slab % 2)


def moved(value, source, target, change):
    pairs = []
    for slab in range(SLABS):
        for tile in range(TILES):
            to_slab, to_tile = change(slab, tile)
            if 0 <= to_slab < SLABS and 0 <= to_tile < TILES:
                pairs.append((source(slab, tile), target(to_slab, to_tile)))
    return lax.ppermute(value, AXES, pairs)


def placed(value):
    return moved(value, given, working, lambda slab, tile: (slab, tile))


def along_slabs(value, step):
    return moved(value, working, working, lambda slab, tile: (slab + step, tile))


def along_tiles(value, step):
    return moved(value, working, working, lambda slab, tile: (slab, tile + step))


def split(value):
    high = value.astype(BF16)
    low = (value - high.astype(F32)).astype(BF16)
    return high, low


def banded(taps, shape, period, axis, shift, low_from):
    i = lax.broadcasted_iota(jnp.int32, shape, 0)
    j = lax.broadcasted_iota(jnp.int32, shape, 1)
    is_low = j >= low_from
    for _ in range(2):
        j = jnp.where(j >= period, j - period, j)
    offset = j - i + shift if axis == 1 else i - j + shift
    value = jnp.zeros(shape, F32)
    for t, tap in enumerate(taps):
        value = jnp.where(offset == t, tap, value)
    high, low = split(value)
    return jnp.where(is_low, low.astype(F32), high.astype(F32)).astype(BF16)


def matrix_kernel(kernels_ref, *outs):
    for v in range(2):
        left, back_left, right, back_right = outs[4 * v : 4 * v + 4]
        rows, tall = left.shape[0], back_left.shape[0]
        width = right.shape[1]
        along_y = [kernels_ref[v, 1, t] for t in range(kernels_ref.shape[2])]
        along_x = [kernels_ref[v, 2, t] for t in range(kernels_ref.shape[2])]
        half = len(along_y) // 2
        left[...] = banded(along_y, left.shape, tall, 1, half - EDGE, 2 * tall)
        back_left[...] = banded(along_y, back_left.shape, rows, 0, half - EDGE, 2 * rows)
        for part in range(2):
            low_from = width * (1 - part)
            right[part] = banded(along_x, right.shape[1:], width, 0, half, low_from)
            back_right[part] = banded(along_x, right.shape[1:], width, 1, half, low_from)


def filter_matrices(kernels, rows, width):
    tall = rows + 2 * EDGE
    shapes = [(rows, 3 * tall), (tall, 3 * rows), (2, width, width), (2, width, width)] * 2
    out = pl.pallas_call(
        matrix_kernel,
        out_shape=[jax.ShapeDtypeStruct(shape, BF16) for shape in shapes],
        in_specs=[pl.BlockSpec(memory_space=pltpu.SMEM)],
        out_specs=[pl.BlockSpec(memory_space=pltpu.VMEM)] * len(shapes),
    )(kernels)
    return out[:4], out[4:]


def gather_planes(taps, planes, depth):
    outs = []
    for z in range(depth):
        total = taps[0] * planes[z]
        for t in range(1, len(taps)):
            total = total + taps[t] * planes[z + t]
        outs.append(total)
    return outs


def scatter_planes(tap_lists, plane_lists):
    depth = len(plane_lists[0])
    count = len(tap_lists[0])
    outs = []
    for o in range(depth + count - 1):
        total = None
        for taps, planes in zip(tap_lists, plane_lists):
            for z in range(max(0, o - count + 1), min(depth, o + 1)):
                term = taps[o - z] * planes[z]
                total = term if total is None else total + term
        outs.append(total)
    return outs


def z_forward(taps, field, out_ref):
    center, z_low, z_high, y_low, y_high = field
    depth, rows, width = center.shape
    reach = z_low.shape[0]

    def strip(first_row, planes_of):
        for lane in range(0, width, 128):
            lanes = pl.ds(lane, 128)
            planes = planes_of(lanes)
            for z, total in enumerate(gather_planes(taps, planes, depth)):
                out_ref[z, pl.ds(first_row, EDGE), lanes] = total

    def inner(step, carry):
        row = pl.multiple_of(step * EDGE, EDGE)

        def planes_of(lanes):
            window = pl.ds(row, EDGE)
            return (
                [z_low[z, window, lanes] for z in range(reach)]
                + [center[z, window, lanes] for z in range(depth)]
                + [z_high[z, window, lanes] for z in range(reach)]
            )

        strip(row + EDGE, planes_of)
        return carry

    lax.fori_loop(0, rows // EDGE, inner, 0)
    strip(0, lambda lanes: [y_low[z, :, lanes] for z in range(depth + 2 * reach)])
    strip(rows + EDGE, lambda lanes: [y_high[z, :, lanes] for z in range(depth + 2 * reach)])


def left_product(matrix, value):
    high, low = split(value)
    stacked = jnp.concatenate([high, low, high], axis=0)
    return jnp.dot(matrix, stacked, preferred_element_type=F32)


def right_product(value, matrix_ref):
    high, low = split(value)
    dot = functools.partial(jnp.dot, preferred_element_type=F32)
    return dot(high, matrix_ref[0]) + dot(low, matrix_ref[0]) + dot(high, matrix_ref[1])


def blurred_chunk(along_z, first, left, right):
    rows = [left_product(left[...], along_z[first + k]) for k in range(CHUNK)]
    return right_product(jnp.concatenate(rows, axis=0), right)


def back_chunk(ratio, first, left, right, out_ref):
    rows = out_ref.shape[1] - 2 * EDGE
    across = right_product(ratio, right)
    for k in range(CHUNK):
        out_ref[first + k] = left_product(left[...], across[k * rows : (k + 1) * rows])


def z_back(tap_lists, sources, outs, extra):
    center, y_low, y_high = outs
    depth = sources[0].shape[0]
    rows, width = center.shape[1:]

    def strip(source_row, out_ref, extra_ref, out_row):
        for lane in range(0, width, 128):
            lanes = pl.ds(lane, 128)
            plane_lists = [
                [ref[z, pl.ds(source_row, EDGE), lanes] for z in range(depth)] for ref in sources
            ]
            for o, total in enumerate(scatter_planes(tap_lists, plane_lists)):
                if extra_ref is not None:
                    total = total + extra_ref[o, pl.ds(out_row, EDGE), lanes]
                out_ref[o, pl.ds(out_row, EDGE), lanes] = total

    def inner(step, carry):
        row = pl.multiple_of(step * EDGE, EDGE)
        strip(row + EDGE, center, extra and extra[0], row)
        return carry

    lax.fori_loop(0, rows // EDGE, inner, 0)
    strip(0, y_low, extra and extra[1], 0)
    strip(rows + EDGE, y_high, extra and extra[2], 0)


def read_taps(ref, view, flip):
    taps = [ref[view, t] for t in range(ref.shape[1])]
    return taps[::-1] if flip else taps


def first_kernel(taps_ref, *refs):
    field, refs = refs[:5], refs[5:]
    view_one = refs[0]
    left_one, back_left_one, right_one, back_right_one, left_two, right_two = refs[1:7]
    partial, blurred_two = refs[7:10], refs[10]
    along_z, back = refs[11:13]
    depth, rows, _ = view_one.shape
    one, two = read_taps(taps_ref, 0, False), read_taps(taps_ref, 1, True)
    z_forward(one, field, along_z)
    for first in range(0, depth, CHUNK):
        blurred = blurred_chunk(along_z, first, left_one, right_one)
        seen = jnp.concatenate([view_one[first + k] for k in range(CHUNK)], axis=0)
        back_chunk(seen / blurred, first, back_left_one, back_right_one, back)
    z_back([one], [back], partial, None)
    z_forward(two, field, along_z)
    for first in range(0, depth, CHUNK):
        blurred = blurred_chunk(along_z, first, left_two, right_two)
        for k in range(CHUNK):
            blurred_two[first + k] = blurred[k * rows : (k + 1) * rows]


def second_kernel(taps_ref, blurred_two, view_two, back_left, back_right, *refs):
    extra, outs, back = refs[:3], refs[3:6], refs[6]
    depth = view_two.shape[0]
    for first in range(0, depth, CHUNK):
        ratio = jnp.concatenate(
            [view_two[depth - 1 - first - k] / blurred_two[first + k] for k in range(CHUNK)],
            axis=0,
        )
        back_chunk(ratio, first, back_left, back_right, back)
    z_back([read_taps(taps_ref, 1, True)], [back], outs, extra)


def both_kernel(taps_ref, *refs):
    field, refs = refs[:5], refs[5:]
    views, refs = refs[:2], refs[2:]
    matrices = (refs[:4], refs[4:8])
    outs, along_z, backs = refs[8:11], refs[11], refs[12:14]
    depth = views[0].shape[0]
    taps = [read_taps(taps_ref, 0, False), read_taps(taps_ref, 1, True)]
    for v in range(2):
        left, back_left, right, back_right = matrices[v]
        z_forward(taps[v], field, along_z)
        for first in range(0, depth, CHUNK):
            blurred = blurred_chunk(along_z, first, left, right)
            planes = [first + k if v == 0 else depth - 1 - first - k for k in range(CHUNK)]
            seen = jnp.concatenate([views[v][z] for z in planes], axis=0)
            back_chunk(seen / blurred, first, back_left, back_right, backs[v])
    z_back(taps, backs, outs, None)


def call(kernel, arrays, outs, scratch):
    vmem = pl.BlockSpec(memory_space=pltpu.VMEM)
    return pl.pallas_call(
        kernel,
        out_shape=[jax.ShapeDtypeStruct(shape, F32) for shape in outs],
        in_specs=[pl.BlockSpec(memory_space=pltpu.SMEM)] + [vmem] * (len(arrays) - 1),
        out_specs=[vmem] * len(outs),
        scratch_shapes=[pltpu.VMEM(shape, F32) for shape in scratch],
    )(*arrays)


def row_halos(center, z_low, z_high):
    def rows(window):
        return jnp.concatenate([z_low[:, window], center[:, window], z_high[:, window]], axis=0)

    low = along_tiles(rows(slice(-EDGE, None)), 1)
    high = along_tiles(rows(slice(None, EDGE)), -1)
    return low, high


def rows_added(partial):
    center, low, high = partial
    from_below = along_tiles(high, 1)
    from_above = along_tiles(low, -1)
    rows = center.shape[1]
    return jnp.concatenate(
        [
            center[:, :EDGE] + from_below,
            center[:, EDGE : rows - EDGE],
            center[:, rows - EDGE :] + from_above,
        ],
        axis=1,
    )


def local(view_one, view_two, estimate, psf):
    depth, rows, width = estimate.shape
    kernels = psf / jnp.sum(psf, axis=2, keepdims=True)
    reach = psf.shape[2] // 2
    z_taps = kernels[:, 0]
    one, two = filter_matrices(kernels, rows, width)
    estimate = placed(estimate)

    z_low = along_slabs(estimate[depth - reach :], 1)
    z_high = along_slabs(estimate[:reach], -1)
    view_two = moved(view_two, given, working, lambda slab, tile: (SLABS - 1 - slab, tile))
    view_one = placed(view_one)

    full = depth + 2 * reach
    partial_shapes = [(full, rows, width), (full, EDGE, width), (full, EDGE, width)]
    tall = (depth, rows + 2 * EDGE, width)

    y_low, y_high = row_halos(estimate, z_low, z_high)
    field = (estimate, z_low, z_high, y_low, y_high)
    *partial, blurred_two = call(
        first_kernel,
        (z_taps, *field, view_one, *one, two[0], two[2]),
        partial_shapes + [view_one.shape],
        [tall, tall],
    )
    partial = call(
        second_kernel,
        (z_taps, blurred_two, view_two, two[1], two[3], *partial),
        partial_shapes,
        [tall],
    )
    total = rows_added(partial)
    overlap = 2 * reach
    below = total[:overlap] + along_slabs(total[full - overlap :], 1)
    above = total[full - overlap :] + along_slabs(total[:overlap], -1)
    z_low = z_low * below[:reach] * 0.5
    z_high = z_high * above[reach:] * 0.5
    estimate = (
        estimate
        * jnp.concatenate([below[reach:], total[overlap : full - overlap], above[:reach]], axis=0)
        * 0.5
    )

    y_low, y_high = row_halos(estimate, z_low, z_high)
    field = (estimate, z_low, z_high, y_low, y_high)
    partial = call(
        both_kernel,
        (z_taps, *field, view_one, view_two, *one, *two),
        partial_shapes,
        [tall, tall, tall],
    )
    total = rows_added(partial)
    from_below = along_slabs(total[full - reach :], 1)
    from_above = along_slabs(total[:reach], -1)
    center = total[reach : full - reach]
    center = jnp.concatenate(
        [
            center[:reach] + from_below,
            center[reach : depth - reach],
            center[depth - reach :] + from_above,
        ],
        axis=0,
    )
    return moved(estimate * center * 0.5, working, given, lambda slab, tile: (slab, tile))


def solution(mesh):
    return jax.shard_map(
        local,
        mesh=mesh,
        in_specs=(P("gz", "xy", None), P("gz", "xy", None), P("gz", "xy", None), P()),
        out_specs=P("gz", "xy", None),
        check_vma=False,
    )
```

```python
import functools

import jax
import jax.numpy as jnp
from jax import lax
from jax.experimental import pallas as pl
from jax.experimental.pallas import tpu as pltpu
from jax.sharding import PartitionSpec as P


EDGE = 8
CHUNK = 4
F32 = jnp.float32
BF16 = jnp.bfloat16


AXES = ("gz", "xy")
SLABS = 16
TILES = 16


def given(slab, tile):
    return slab * TILES + tile


def working(slab, tile):
    return given(slab - slab % 2 + tile % 2, tile - tile % 2 + slab % 2)


def moved(value, source, target, change):
    pairs = []
    for slab in range(SLABS):
        for tile in range(TILES):
            to_slab, to_tile = change(slab, tile)
            if 0 <= to_slab < SLABS and 0 <= to_tile < TILES:
                pairs.append((source(slab, tile), target(to_slab, to_tile)))
    return lax.ppermute(value, AXES, pairs)


def placed(value):
    return moved(value, given, working, lambda slab, tile: (slab, tile))


def along_slabs(value, step):
    return moved(value, working, working, lambda slab, tile: (slab + step, tile))


def along_tiles(value, step):
    return moved(value, working, working, lambda slab, tile: (slab, tile + step))


def split(value):
    high = value.astype(BF16)
    low = (value - high.astype(F32)).astype(BF16)
    return high, low


def banded(taps, shape, period, axis, shift, low_from):
    i = lax.broadcasted_iota(jnp.int32, shape, 0)
    j = lax.broadcasted_iota(jnp.int32, shape, 1)
    is_low = j >= low_from
    for _ in range(2):
        j = jnp.where(j >= period, j - period, j)
    offset = j - i + shift if axis == 1 else i - j + shift
    value = jnp.zeros(shape, F32)
    for t, tap in enumerate(taps):
        value = jnp.where(offset == t, tap, value)
    high, low = split(value)
    return jnp.where(is_low, low.astype(F32), high.astype(F32)).astype(BF16)


def matrix_kernel(kernels_ref, *outs):
    for v in range(2):
        left, back_left, right, back_right = outs[4 * v : 4 * v + 4]
        rows, tall = left.shape[0], back_left.shape[0]
        width = right.shape[1]
        along_y = [kernels_ref[v, 1, t] for t in range(kernels_ref.shape[2])]
        along_x = [kernels_ref[v, 2, t] for t in range(kernels_ref.shape[2])]
        half = len(along_y) // 2
        left[...] = banded(along_y, left.shape, tall, 1, half - EDGE, 2 * tall)
        back_left[...] = banded(along_y, back_left.shape, rows, 0, half - EDGE, 2 * rows)
        for part in range(2):
            low_from = width * (1 - part)
            right[part] = banded(along_x, right.shape[1:], width, 0, half, low_from)
            back_right[part] = banded(along_x, right.shape[1:], width, 1, half, low_from)


def filter_matrices(kernels, rows, width):
    tall = rows + 2 * EDGE
    shapes = [(rows, 3 * tall), (tall, 3 * rows), (2, width, width), (2, width, width)] * 2
    out = pl.pallas_call(
        matrix_kernel,
        out_shape=[jax.ShapeDtypeStruct(shape, BF16) for shape in shapes],
        in_specs=[pl.BlockSpec(memory_space=pltpu.SMEM)],
        out_specs=[pl.BlockSpec(memory_space=pltpu.VMEM)] * len(shapes),
    )(kernels)
    return out[:4], out[4:]


def gather_planes(taps, planes, depth):
    outs = []
    for z in range(depth):
        total = taps[0] * planes[z]
        for t in range(1, len(taps)):
            total = total + taps[t] * planes[z + t]
        outs.append(total)
    return outs


def scatter_planes(tap_lists, plane_lists):
    depth = len(plane_lists[0])
    count = len(tap_lists[0])
    outs = []
    for o in range(depth + count - 1):
        total = None
        for taps, planes in zip(tap_lists, plane_lists):
            for z in range(max(0, o - count + 1), min(depth, o + 1)):
                term = taps[o - z] * planes[z]
                total = term if total is None else total + term
        outs.append(total)
    return outs


def z_forward(taps, extended, out_ref):
    depth, rows, width = out_ref.shape

    def strip(step, carry):
        window = pl.ds(pl.multiple_of(step * EDGE, EDGE), EDGE)
        for lane in range(0, width, 128):
            lanes = pl.ds(lane, 128)
            planes = [extended[z, window, lanes] for z in range(extended.shape[0])]
            for z, total in enumerate(gather_planes(taps, planes, depth)):
                out_ref[z, window, lanes] = total
        return carry

    lax.fori_loop(0, rows // EDGE, strip, 0)


def left_product(matrix, value):
    high, low = split(value)
    stacked = jnp.concatenate([high, low, high], axis=0)
    return jnp.dot(matrix, stacked, preferred_element_type=F32)


def right_product(value, matrix_ref):
    high, low = split(value)
    dot = functools.partial(jnp.dot, preferred_element_type=F32)
    return dot(high, matrix_ref[0]) + dot(low, matrix_ref[0]) + dot(high, matrix_ref[1])


def blurred_chunk(along_z, first, left, right):
    rows = [left_product(left[...], along_z[first + k]) for k in range(CHUNK)]
    return right_product(jnp.concatenate(rows, axis=0), right)


def back_chunk(ratio, first, left, right, out_ref):
    rows = out_ref.shape[1] - 2 * EDGE
    across = right_product(ratio, right)
    for k in range(CHUNK):
        out_ref[first + k] = left_product(left[...], across[k * rows : (k + 1) * rows])


def z_back(tap_lists, sources, segments):
    depth, _, width = sources[0].shape

    for first, count, store in segments:

        def strip(step, carry, first=first, store=store):
            row = pl.multiple_of(step * EDGE, EDGE)
            for lane in range(0, width, 128):
                lanes = pl.ds(lane, 128)
                window = pl.ds(row + first * EDGE, EDGE)
                plane_lists = [[ref[z, window, lanes] for z in range(depth)] for ref in sources]
                for o, total in enumerate(scatter_planes(tap_lists, plane_lists)):
                    store(o, row, lanes, total)
            return carry

        lax.fori_loop(0, count, strip, 0)


def read_taps(ref, view, flip):
    taps = [ref[view, t] for t in range(ref.shape[1])]
    return taps[::-1] if flip else taps


def blur_into(out_ref, taps, extended, along_z, left, right):
    depth, rows, _ = out_ref.shape
    z_forward(taps, extended, along_z)
    for first in range(0, depth, CHUNK):
        blurred = blurred_chunk(along_z, first, left, right)
        for k in range(CHUNK):
            out_ref[first + k] = blurred[k * rows : (k + 1) * rows]


def ratios_back(seen_planes, blurred, left, right, back):
    for first in range(0, blurred.shape[0], CHUNK):
        ratio = jnp.concatenate(
            [seen_planes[first + k] / blurred[first + k] for k in range(CHUNK)], axis=0
        )
        back_chunk(ratio, first, left, right, back)


class Mirrored:
    def __init__(self, low_half, high_half):
        planes = [(half, z) for half in (low_half, high_half) for z in range(half.shape[0])]
        self.planes = planes[::-1]

    def __getitem__(self, index):
        half, z = self.planes[index]
        return half[z]


def forward_kernel(taps_ref, *refs):
    center, z_low, z_high, y_low, y_high = refs[:5]
    mats = refs[5:9]
    extended, blurred, along_z = refs[9], refs[10:12], refs[12]
    depth, rows, _ = center.shape
    reach = z_low.shape[0]
    inner = pl.ds(EDGE, rows)
    extended[:reach, inner] = z_low[...]
    extended[pl.ds(reach, depth), inner] = center[...]
    extended[pl.ds(reach + depth, reach), inner] = z_high[...]
    extended[:, :EDGE] = y_low[...]
    extended[:, pl.ds(EDGE + rows, EDGE)] = y_high[...]
    for v in range(2):
        taps = read_taps(taps_ref, v, v == 1)
        blur_into(blurred[v], taps, extended, along_z, mats[2 * v], mats[2 * v + 1])


def back_kernel(taps_ref, *refs):
    blurred, view_one, halves, mats = refs[:2], refs[2], refs[3:5], refs[5:9]
    y_low, y_mid, y_high = refs[9:12]
    backs = refs[12:14]
    ratios_back(view_one, blurred[0], mats[0], mats[1], backs[0])
    ratios_back(Mirrored(*halves), blurred[1], mats[2], mats[3], backs[1])
    segments = []
    first = 0
    for ref in (y_low, y_mid, y_high):

        def store(o, row, lanes, total, ref=ref):
            ref[o, pl.ds(row, EDGE), lanes] = total

        segments.append((first, ref.shape[1] // EDGE, store))
        first += ref.shape[1] // EDGE
    z_back([read_taps(taps_ref, 0, False), read_taps(taps_ref, 1, True)], backs, segments)


def row_sum_kernel(y_low, y_mid, y_high, from_below, from_above, z_low, z_mid, z_high):
    edge, inner = y_low.shape[1], y_mid.shape[1]
    first = 0
    for ref in (z_low, z_mid, z_high):
        planes = pl.ds(first, ref.shape[0])
        ref[:, :edge] = y_low[planes] + from_below[planes]
        ref[:, pl.ds(edge, inner)] = y_mid[planes]
        ref[:, pl.ds(edge + inner, edge)] = y_high[planes] + from_above[planes]
        first += ref.shape[0]


def second_kernel(taps_ref, *refs):
    before, z_low, z_mid, z_high, from_below, from_above = refs[:6]
    view_one, halves, mats = refs[6], refs[7:9], refs[9:17]
    y_low_out, y_high_out, z_low_out, z_mid_out, z_high_out = refs[17:22]
    estimate, along_z, backs = refs[22], refs[23], refs[24:26]
    overlap, middle = z_low.shape[0], z_mid.shape[0]
    for o in range(before.shape[0]):
        if o < overlap:
            total = z_low[o] + from_below[o]
        elif o < overlap + middle:
            total = z_mid[o - overlap]
        else:
            total = z_high[o - overlap - middle] + from_above[o - overlap - middle]
        estimate[o] = before[o] * total * 0.5
    taps = [read_taps(taps_ref, 0, False), read_taps(taps_ref, 1, True)]
    seen = (view_one, Mirrored(*halves))
    for v in range(2):
        left, back_left, right, back_right = mats[4 * v : 4 * v + 4]
        z_forward(taps[v], estimate, along_z)
        for first in range(0, view_one.shape[0], CHUNK):
            blurred = blurred_chunk(along_z, first, left, right)
            ratio = jnp.concatenate([seen[v][first + k] for k in range(CHUNK)], axis=0) / blurred
            back_chunk(ratio, first, back_left, back_right, backs[v])
    rows = z_mid_out.shape[1]
    reach = z_low_out.shape[0]
    depth = z_mid_out.shape[0]

    def scaled(o, row, lanes, total):
        return total * estimate[o, pl.ds(row, EDGE), lanes] * 0.5

    def store_low(o, row, lanes, total):
        y_low_out[o, :, lanes] = scaled(o, 0, lanes, total)

    def store_high(o, row, lanes, total):
        y_high_out[o, :, lanes] = scaled(o, rows + EDGE, lanes, total)

    def store_inner(o, row, lanes, total):
        value = scaled(o, pl.multiple_of(row + EDGE, EDGE), lanes, total)
        if o < reach:
            ref, plane = z_low_out, o
        elif o < reach + depth:
            ref, plane = z_mid_out, o - reach
        else:
            ref, plane = z_high_out, o - reach - depth
        ref[plane, pl.ds(row, EDGE), lanes] = value

    strips = rows // EDGE
    z_back(
        taps, backs, [(0, 1, store_low), (1, strips, store_inner), (strips + 1, 1, store_high)]
    )


def last_row_sum_kernel(z_low, z_mid, z_high, from_below, from_above, *outs):
    first = 0
    for ref, out in zip((z_low, z_mid, z_high), outs):
        planes = pl.ds(first, ref.shape[0])
        rows = ref.shape[1]
        out[:, :EDGE] = ref[:, :EDGE] + from_below[planes]
        out[:, pl.ds(EDGE, rows - 2 * EDGE)] = ref[:, pl.ds(EDGE, rows - 2 * EDGE)]
        tail = pl.ds(rows - EDGE, EDGE)
        out[:, tail] = ref[:, tail] + from_above[planes]
        first += ref.shape[0]


def call(kernel, arrays, outs, scratch=(), scalars=1):
    vmem = pl.BlockSpec(memory_space=pltpu.VMEM)
    smem = pl.BlockSpec(memory_space=pltpu.SMEM)
    return pl.pallas_call(
        kernel,
        out_shape=[jax.ShapeDtypeStruct(shape, F32) for shape in outs],
        in_specs=[smem] * scalars + [vmem] * (len(arrays) - scalars),
        out_specs=[vmem] * len(outs),
        scratch_shapes=[pltpu.VMEM(shape, F32) for shape in scratch],
    )(*arrays)


def local(view_one, view_two, estimate, psf):
    depth, rows, width = estimate.shape
    kernels = psf / jnp.sum(psf, axis=2, keepdims=True)
    reach = psf.shape[2] // 2
    z_taps = kernels[:, 0]
    one, two = filter_matrices(kernels, rows, width)
    full = depth + 2 * reach
    half = depth // 2

    def mirror(value):
        return moved(value, given, working, lambda slab, tile: (SLABS - 1 - slab, tile))

    estimate = placed(estimate)
    first_half = mirror(view_two[:half])
    z_low = along_slabs(estimate[depth - reach :], 1)
    z_high = along_slabs(estimate[:reach], -1)
    second_half = mirror(view_two[half:])

    def rows_of(window):
        return jnp.concatenate([z_low[:, window], estimate[:, window], z_high[:, window]], axis=0)

    y_low = along_tiles(rows_of(slice(-EDGE, None)), 1)
    y_high = along_tiles(rows_of(slice(None, EDGE)), -1)
    view_one = placed(view_one)

    tall = (depth, rows + 2 * EDGE, width)
    extended = (full, rows + 2 * EDGE, width)
    before, *blurred = call(
        forward_kernel,
        (z_taps, estimate, z_low, z_high, y_low, y_high, one[0], one[2], two[0], two[2]),
        [extended, view_one.shape, view_one.shape],
        [tall],
    )
    y_low, y_mid, y_high = call(
        back_kernel,
        (z_taps, *blurred, view_one, first_half, second_half, one[1], one[3], two[1], two[3]),
        [(full, 2 * EDGE, width), (full, rows - 2 * EDGE, width), (full, 2 * EDGE, width)],
        [tall, tall],
    )
    from_below = along_tiles(y_high, 1)
    from_above = along_tiles(y_low, -1)
    overlap = 2 * reach
    z_low, z_mid, z_high = call(
        row_sum_kernel,
        (y_low, y_mid, y_high, from_below, from_above),
        [(n, rows + 2 * EDGE, width) for n in (overlap, full - 2 * overlap, overlap)],
        scalars=0,
    )
    from_below = along_slabs(z_high, 1)
    from_above = along_slabs(z_low, -1)
    y_low, y_high, *pieces = call(
        second_kernel,
        (z_taps, before, z_low, z_mid, z_high, from_below, from_above)
        + (view_one, first_half, second_half, *one, *two),
        [(full, EDGE, width)] * 2 + [(n, rows, width) for n in (reach, depth, reach)],
        [extended, tall, tall, tall],
    )
    from_below = along_tiles(y_high, 1)
    from_above = along_tiles(y_low, -1)
    z_low, z_mid, z_high = call(
        last_row_sum_kernel,
        (*pieces, from_below, from_above),
        [piece.shape for piece in pieces],
        scalars=0,
    )
    center = moved(z_mid, working, given, lambda slab, tile: (slab, tile))
    from_below = moved(z_high, working, given, lambda slab, tile: (slab + 1, tile))
    from_above = moved(z_low, working, given, lambda slab, tile: (slab - 1, tile))
    return jnp.concatenate(
        [
            center[:reach] + from_below,
            center[reach : depth - reach],
            center[depth - reach :] + from_above,
        ],
        axis=0,
    )


def solution(mesh):
    return jax.shard_map(
        local,
        mesh=mesh,
        in_specs=(P("gz", "xy", None), P("gz", "xy", None), P("gz", "xy", None), P()),
        out_specs=P("gz", "xy", None),
        check_vma=False,
    )
```

```python
import functools

import jax
import jax.numpy as jnp
from jax import lax
from jax.experimental import pallas as pl
from jax.experimental.pallas import tpu as pltpu
from jax.sharding import PartitionSpec as P


EDGE = 8
CHUNK = 4
LIMIT = 24 << 20
F32 = jnp.float32
BF16 = jnp.bfloat16


AXES = ("gz", "xy")
SLABS = 16
TILES = 16


def given(slab, tile):
    return slab * TILES + tile


def working(slab, tile):
    column, step = divmod(tile, 4)
    if column % 2:
        step = 3 - step
    return given(slab - slab % 2 + step // 2, 4 * column + 2 * (step % 2) + slab % 2)


def moved(value, source, target, change):
    pairs = []
    for slab in range(SLABS):
        for tile in range(TILES):
            to_slab, to_tile = change(slab, tile)
            if 0 <= to_slab < SLABS and 0 <= to_tile < TILES:
                pairs.append((source(slab, tile), target(to_slab, to_tile)))
    return lax.ppermute(value, AXES, pairs)


def along_slabs(value, step):
    return moved(value, working, working, lambda slab, tile: (slab + step, tile))


def along_tiles(value, step):
    return moved(value, working, working, lambda slab, tile: (slab, tile + step))


def split(value):
    high = value.astype(BF16)
    low = (value - high.astype(F32)).astype(BF16)
    return high, low


def banded(taps, shape, period, axis, shift, low_from):
    i = lax.broadcasted_iota(jnp.int32, shape, 0)
    j = lax.broadcasted_iota(jnp.int32, shape, 1)
    is_low = j >= low_from
    for _ in range(2):
        j = jnp.where(j >= period, j - period, j)
    offset = j - i + shift if axis == 1 else i - j + shift
    value = jnp.zeros(shape, F32)
    for t, tap in enumerate(taps):
        value = jnp.where(offset == t, tap, value)
    high, low = split(value)
    return jnp.where(is_low, low.astype(F32), high.astype(F32)).astype(BF16)


def matrix_kernel(kernels_ref, *outs):
    for v in range(2):
        left, back_left, right, back_right = outs[4 * v : 4 * v + 4]
        rows, tall = left.shape[0], back_left.shape[0]
        width = right.shape[1]
        along_y = [kernels_ref[v, 1, t] for t in range(kernels_ref.shape[2])]
        along_x = [kernels_ref[v, 2, t] for t in range(kernels_ref.shape[2])]
        half = len(along_y) // 2
        left[...] = banded(along_y, left.shape, tall, 1, half - EDGE, 2 * tall)
        back_left[...] = banded(along_y, back_left.shape, rows, 0, half - EDGE, 2 * rows)
        for part in range(2):
            low_from = width * (1 - part)
            right[part] = banded(along_x, right.shape[1:], width, 0, half, low_from)
            back_right[part] = banded(along_x, right.shape[1:], width, 1, half, low_from)


def filter_matrices(kernels, rows, width):
    tall = rows + 2 * EDGE
    shapes = [(rows, 3 * tall), (tall, 3 * rows), (2, width, width), (2, width, width)] * 2
    out = pl.pallas_call(
        matrix_kernel,
        out_shape=[jax.ShapeDtypeStruct(shape, BF16) for shape in shapes],
        in_specs=[pl.BlockSpec(memory_space=pltpu.SMEM)],
        out_specs=[pl.BlockSpec(memory_space=pltpu.VMEM)] * len(shapes),
    )(kernels)
    return out[:4], out[4:]


def gather_planes(taps, planes, depth):
    outs = []
    for z in range(depth):
        total = taps[0] * planes[z]
        for t in range(1, len(taps)):
            total = total + taps[t] * planes[z + t]
        outs.append(total)
    return outs


def scatter_planes(tap_lists, plane_lists):
    depth = len(plane_lists[0])
    count = len(tap_lists[0])
    outs = []
    for o in range(depth + count - 1):
        total = None
        for taps, planes in zip(tap_lists, plane_lists):
            for z in range(max(0, o - count + 1), min(depth, o + 1)):
                term = taps[o - z] * planes[z]
                total = term if total is None else total + term
        outs.append(total)
    return outs


def z_forward(taps, extended, out_ref):
    depth, rows, width = out_ref.shape

    def strip(step, carry):
        window = pl.ds(pl.multiple_of(step * EDGE, EDGE), EDGE)
        for lane in range(0, width, 128):
            lanes = pl.ds(lane, 128)
            planes = [extended[z, window, lanes] for z in range(extended.shape[0])]
            for z, total in enumerate(gather_planes(taps, planes, depth)):
                out_ref[z, window, lanes] = total
        return carry

    lax.fori_loop(0, rows // EDGE, strip, 0)


def left_product(matrix, value):
    high, low = split(value)
    stacked = jnp.concatenate([high, low, high], axis=0)
    return jnp.dot(matrix, stacked, preferred_element_type=F32)


def right_product(value, matrix_ref):
    high, low = split(value)
    dot = functools.partial(jnp.dot, preferred_element_type=F32)
    return dot(high, matrix_ref[0]) + dot(low, matrix_ref[0]) + dot(high, matrix_ref[1])


def blurred_chunk(along_z, first, left, right):
    rows = [left_product(left[...], along_z[first + k]) for k in range(CHUNK)]
    return right_product(jnp.concatenate(rows, axis=0), right)


def back_chunk(ratio, first, left, right, out_ref):
    rows = out_ref.shape[1] - 2 * EDGE
    across = right_product(ratio, right)
    for k in range(CHUNK):
        out_ref[first + k] = left_product(left[...], across[k * rows : (k + 1) * rows])


def z_back(tap_lists, sources, segments):
    depth, _, width = sources[0].shape

    for first, count, store in segments:

        def strip(step, carry, first=first, store=store):
            row = pl.multiple_of(step * EDGE, EDGE)
            for lane in range(0, width, 128):
                lanes = pl.ds(lane, 128)
                window = pl.ds(row + first * EDGE, EDGE)
                plane_lists = [[ref[z, window, lanes] for z in range(depth)] for ref in sources]
                for o, total in enumerate(scatter_planes(tap_lists, plane_lists)):
                    store(o, row, lanes, total)
            return carry

        lax.fori_loop(0, count, strip, 0)


def read_taps(ref, view, flip):
    taps = [ref[view, t] for t in range(ref.shape[1])]
    return taps[::-1] if flip else taps


def blur_into(out_ref, taps, extended, along_z, left, right):
    depth, rows, _ = out_ref.shape
    z_forward(taps, extended, along_z)
    for first in range(0, depth, CHUNK):
        blurred = blurred_chunk(along_z, first, left, right)
        for k in range(CHUNK):
            out_ref[first + k] = blurred[k * rows : (k + 1) * rows]


def ratios_back(seen_planes, blurred, left, right, back):
    for first in range(0, blurred.shape[0], CHUNK):
        ratio = jnp.concatenate(
            [seen_planes[first + k] / blurred[first + k] for k in range(CHUNK)], axis=0
        )
        back_chunk(ratio, first, left, right, back)


class Mirrored:
    def __init__(self, low_half, high_half):
        planes = [(ref, z) for ref in (low_half, high_half) for z in range(ref.shape[0])]
        self.planes = planes[::-1]

    def __getitem__(self, index):
        ref, z = self.planes[index]
        return ref[z]


def forward_kernel(taps_ref, *refs):
    center, z_low, z_high, y_low, y_high = refs[:5]
    mats = refs[5:9]
    extended, blurred, along_z = refs[9], refs[10:12], refs[12]
    depth, rows, _ = center.shape
    reach = z_low.shape[0]
    inner = pl.ds(EDGE, rows)
    extended[:reach, inner] = z_low[...]
    extended[pl.ds(reach, depth), inner] = center[...]
    extended[pl.ds(reach + depth, reach), inner] = z_high[...]
    extended[:, :EDGE] = y_low[...]
    extended[:, pl.ds(EDGE + rows, EDGE)] = y_high[...]
    for v in range(2):
        taps = read_taps(taps_ref, v, v == 1)
        blur_into(blurred[v], taps, extended, along_z, mats[2 * v], mats[2 * v + 1])


def back_kernel(taps_ref, *refs):
    blurred, view_one, halves, mats = refs[:2], refs[2], refs[3:5], refs[5:9]
    y_low, y_mid, y_high = refs[9:12]
    backs = refs[12:14]
    ratios_back(view_one, blurred[0], mats[0], mats[1], backs[0])
    ratios_back(Mirrored(*halves), blurred[1], mats[2], mats[3], backs[1])
    segments = []
    first = 0
    for ref in (y_low, y_mid, y_high):

        def store(o, row, lanes, total, ref=ref):
            ref[o, pl.ds(row, EDGE), lanes] = total

        segments.append((first, ref.shape[1] // EDGE, store))
        first += ref.shape[1] // EDGE
    z_back([read_taps(taps_ref, 0, False), read_taps(taps_ref, 1, True)], backs, segments)


def row_sum_kernel(y_low, y_mid, y_high, from_below, from_above, z_low, z_mid, z_high):
    edge, inner = y_low.shape[1], y_mid.shape[1]
    first = 0
    for ref in (z_low, z_mid, z_high):
        planes = pl.ds(first, ref.shape[0])
        ref[:, :edge] = y_low[planes] + from_below[planes]
        ref[:, pl.ds(edge, inner)] = y_mid[planes]
        ref[:, pl.ds(edge + inner, edge)] = y_high[planes] + from_above[planes]
        first += ref.shape[0]


def second_kernel(taps_ref, *refs):
    before, z_low, z_mid, z_high, from_below, from_above = refs[:6]
    view_one, halves, mats = refs[6], refs[7:9], refs[9:17]
    y_low_out, y_high_out, z_low_out, z_mid_out, z_high_out = refs[17:22]
    estimate, along_z, backs = refs[22], refs[23], refs[24:26]
    overlap, middle = z_low.shape[0], z_mid.shape[0]
    for o in range(before.shape[0]):
        if o < overlap:
            total = z_low[o] + from_below[o]
        elif o < overlap + middle:
            total = z_mid[o - overlap]
        else:
            total = z_high[o - overlap - middle] + from_above[o - overlap - middle]
        estimate[o] = before[o] * total * 0.5
    taps = [read_taps(taps_ref, 0, False), read_taps(taps_ref, 1, True)]
    seen = (view_one, Mirrored(*halves))
    for v in range(2):
        left, back_left, right, back_right = mats[4 * v : 4 * v + 4]
        z_forward(taps[v], estimate, along_z)
        for first in range(0, view_one.shape[0], CHUNK):
            blurred = blurred_chunk(along_z, first, left, right)
            ratio = jnp.concatenate([seen[v][first + k] for k in range(CHUNK)], axis=0) / blurred
            back_chunk(ratio, first, back_left, back_right, backs[v])
    rows = z_mid_out.shape[1]
    reach = z_low_out.shape[0]
    depth = z_mid_out.shape[0]

    def scaled(o, row, lanes, total):
        return total * estimate[o, pl.ds(row, EDGE), lanes] * 0.5

    def store_low(o, row, lanes, total):
        y_low_out[o, :, lanes] = scaled(o, 0, lanes, total)

    def store_high(o, row, lanes, total):
        y_high_out[o, :, lanes] = scaled(o, rows + EDGE, lanes, total)

    def store_inner(o, row, lanes, total):
        value = scaled(o, pl.multiple_of(row + EDGE, EDGE), lanes, total)
        if o < reach:
            ref, plane = z_low_out, o
        elif o < reach + depth:
            ref, plane = z_mid_out, o - reach
        else:
            ref, plane = z_high_out, o - reach - depth
        ref[plane, pl.ds(row, EDGE), lanes] = value

    strips = rows // EDGE
    z_back(
        taps, backs, [(0, 1, store_low), (1, strips, store_inner), (strips + 1, 1, store_high)]
    )


def last_row_sum_kernel(z_low, z_mid, z_high, from_below, from_above, *outs):
    first = 0
    for ref, out in zip((z_low, z_mid, z_high), outs):
        planes = pl.ds(first, ref.shape[0])
        rows = ref.shape[1]
        out[:, :EDGE] = ref[:, :EDGE] + from_below[planes]
        out[:, pl.ds(EDGE, rows - 2 * EDGE)] = ref[:, pl.ds(EDGE, rows - 2 * EDGE)]
        tail = pl.ds(rows - EDGE, EDGE)
        out[:, tail] = ref[:, tail] + from_above[planes]
        first += ref.shape[0]


def call(kernel, arrays, outs, scratch=(), scalars=1):
    vmem = pl.BlockSpec(memory_space=pltpu.VMEM)
    smem = pl.BlockSpec(memory_space=pltpu.SMEM)
    return pl.pallas_call(
        kernel,
        out_shape=[jax.ShapeDtypeStruct(shape, F32) for shape in outs],
        in_specs=[smem] * scalars + [vmem] * (len(arrays) - scalars),
        out_specs=[vmem] * len(outs),
        scratch_shapes=[pltpu.VMEM(shape, F32) for shape in scratch],
        compiler_params=pltpu.CompilerParams(vmem_limit_bytes=LIMIT),
    )(*arrays)


def local(view_one, view_two, estimate, psf):
    depth, rows, width = estimate.shape
    kernels = psf / jnp.sum(psf, axis=2, keepdims=True)
    reach = psf.shape[2] // 2
    z_taps = kernels[:, 0]
    one, two = filter_matrices(kernels, rows, width)
    full = depth + 2 * reach

    def same(slab, tile):
        return slab, tile

    def across(slab, tile):
        return SLABS - 1 - slab, tile

    half = depth // 2
    first_half = moved(view_two[:half], given, working, across)
    z_low = moved(estimate[depth - reach :], given, working, lambda s, t: (s + 1, t))
    z_high = moved(estimate[:reach], given, working, lambda s, t: (s - 1, t))
    second_half = moved(view_two[half:], given, working, across)
    estimate = moved(estimate, given, working, same)

    def rows_of(window):
        return jnp.concatenate([z_low[:, window], estimate[:, window], z_high[:, window]], axis=0)

    y_low = along_tiles(rows_of(slice(-EDGE, None)), 1)
    y_high = along_tiles(rows_of(slice(None, EDGE)), -1)
    view_one = moved(view_one, given, working, same)

    tall = (depth, rows + 2 * EDGE, width)
    extended = (full, rows + 2 * EDGE, width)
    before, *blurred = call(
        forward_kernel,
        (z_taps, estimate, z_low, z_high, y_low, y_high, one[0], one[2], two[0], two[2]),
        [extended, view_one.shape, view_one.shape],
        [tall],
    )
    y_low, y_mid, y_high = call(
        back_kernel,
        (z_taps, *blurred, view_one, first_half, second_half, one[1], one[3], two[1], two[3]),
        [(full, 2 * EDGE, width), (full, rows - 2 * EDGE, width), (full, 2 * EDGE, width)],
        [tall, tall],
    )
    from_below = along_tiles(y_high, 1)
    from_above = along_tiles(y_low, -1)
    overlap = 2 * reach
    z_low, z_mid, z_high = call(
        row_sum_kernel,
        (y_low, y_mid, y_high, from_below, from_above),
        [(n, rows + 2 * EDGE, width) for n in (overlap, full - 2 * overlap, overlap)],
        scalars=0,
    )
    from_below = along_slabs(z_high, 1)
    from_above = along_slabs(z_low, -1)
    y_low, y_high, *pieces = call(
        second_kernel,
        (z_taps, before, z_low, z_mid, z_high, from_below, from_above)
        + (view_one, first_half, second_half, *one, *two),
        [(full, EDGE, width)] * 2 + [(n, rows, width) for n in (reach, depth, reach)],
        [extended, tall, tall, tall],
    )
    from_below = along_tiles(y_high, 1)
    from_above = along_tiles(y_low, -1)
    z_low, z_mid, z_high = call(
        last_row_sum_kernel,
        (*pieces, from_below, from_above),
        [piece.shape for piece in pieces],
        scalars=0,
    )
    from_below = along_slabs(z_high, 1)
    from_above = along_slabs(z_low, -1)
    result = jnp.concatenate(
        [
            z_mid[:reach] + from_below,
            z_mid[reach : depth - reach],
            z_mid[depth - reach :] + from_above,
        ],
        axis=0,
    )
    return moved(result, working, given, same)


def solution(mesh):
    return jax.shard_map(
        local,
        mesh=mesh,
        in_specs=(P("gz", "xy", None), P("gz", "xy", None), P("gz", "xy", None), P()),
        out_specs=P("gz", "xy", None),
        check_vma=False,
    )
```

```python
import functools

import jax
import jax.numpy as jnp
from jax import lax
from jax.experimental import pallas as pl
from jax.experimental.pallas import tpu as pltpu
from jax.sharding import PartitionSpec as P


EDGE = 8
CHUNK = 16
LIMIT = 12 << 20
PART = 10
F32 = jnp.float32
BF16 = jnp.bfloat16


AXES = ("gz", "xy")
SLABS = 16
TILES = 16


def given(slab, tile):
    return slab * TILES + tile


def working(slab, tile):
    column, step = divmod(tile, 4)
    if column % 2:
        step = 3 - step
    return given(slab - slab % 2 + step // 2, 4 * column + 2 * (step % 2) + slab % 2)


def moved(value, source, target, change):
    pairs = []
    for slab in range(SLABS):
        for tile in range(TILES):
            to_slab, to_tile = change(slab, tile)
            if 0 <= to_slab < SLABS and 0 <= to_tile < TILES:
                pairs.append((source(slab, tile), target(to_slab, to_tile)))
    return lax.ppermute(value, AXES, pairs)


def to_other_core(value):
    return moved(value, working, working, lambda slab, tile: (slab + 1 - slab % 2 * 2, tile))


def to_other_chip(value):
    return moved(value, working, working, lambda slab, tile: (slab - 1 + slab % 2 * 2, tile))


def along_tiles(value, step):
    return moved(value, working, working, lambda slab, tile: (slab, tile + step))


def split(value):
    high = value.astype(BF16)
    low = (value - high.astype(F32)).astype(BF16)
    return high, low


def banded(taps, shape, period, axis, shift, low_from):
    i = lax.broadcasted_iota(jnp.int32, shape, 0)
    j = lax.broadcasted_iota(jnp.int32, shape, 1)
    is_low = j >= low_from
    for _ in range(2):
        j = jnp.where(j >= period, j - period, j)
    offset = j - i + shift if axis == 1 else i - j + shift
    value = jnp.zeros(shape, F32)
    for t, tap in enumerate(taps):
        value = jnp.where(offset == t, tap, value)
    value = value / jnp.full(shape, sum(taps), F32)
    high, low = split(value)
    return jnp.where(is_low, low.astype(F32), high.astype(F32)).astype(BF16)


def matrix_kernel(kernels_ref, *outs):
    for v in range(2):
        left, back_left, right, back_right = outs[4 * v : 4 * v + 4]
        rows, tall = left.shape[0], back_left.shape[0]
        width = right.shape[1]
        along_y = [kernels_ref[v, 1, t] for t in range(kernels_ref.shape[2])]
        along_x = [kernels_ref[v, 2, t] for t in range(kernels_ref.shape[2])]
        half = len(along_y) // 2
        left[...] = banded(along_y, left.shape, tall, 1, half - EDGE, 2 * tall)
        back_left[...] = banded(along_y, back_left.shape, rows, 0, half - EDGE, 2 * rows)
        for part in range(2):
            low_from = width * (1 - part)
            right[part] = banded(along_x, right.shape[1:], width, 0, half, low_from)
            back_right[part] = banded(along_x, right.shape[1:], width, 1, half, low_from)


def filter_matrices(kernels, rows, width):
    tall = rows + 2 * EDGE
    shapes = [(rows, 3 * tall), (tall, 3 * rows), (2, width, width), (2, width, width)] * 2
    out = pl.pallas_call(
        matrix_kernel,
        out_shape=[jax.ShapeDtypeStruct(shape, BF16) for shape in shapes],
        in_specs=[pl.BlockSpec(memory_space=pltpu.SMEM)],
        out_specs=[pl.BlockSpec(memory_space=pltpu.VMEM)] * len(shapes),
        compiler_params=pltpu.CompilerParams(vmem_limit_bytes=LIMIT),
    )(kernels)
    return out[:4], out[4:]


def gather_planes(taps, planes, depth):
    outs = []
    for z in range(depth):
        total = taps[0] * planes[z]
        for t in range(1, len(taps)):
            total = total + taps[t] * planes[z + t]
        outs.append(total)
    return outs


def scatter_planes(tap_lists, plane_lists):
    depth = len(plane_lists[0])
    count = len(tap_lists[0])
    outs = []
    for o in range(depth + count - 1):
        total = None
        for taps, planes in zip(tap_lists, plane_lists):
            for z in range(max(0, o - count + 1), min(depth, o + 1)):
                term = taps[o - z] * planes[z]
                total = term if total is None else total + term
        outs.append(total)
    return outs


def z_forward(taps, extended, out_ref):
    depth, rows, width = out_ref.shape

    def strip(step, carry):
        window = pl.ds(pl.multiple_of(step * EDGE, EDGE), EDGE)
        for lane in range(0, width, 128):
            lanes = pl.ds(lane, 128)
            planes = [extended[z, window, lanes] for z in range(extended.shape[0])]
            for z, total in enumerate(gather_planes(taps, planes, depth)):
                out_ref[z, window, lanes] = total
        return carry

    lax.fori_loop(0, rows // EDGE, strip, 0)


def left_product(matrix, value):
    high, low = split(value)
    stacked = jnp.concatenate([high, low, high], axis=0)
    return jnp.dot(matrix, stacked, preferred_element_type=F32)


def right_product(value, matrix_ref):
    high, low = split(value)
    dot = functools.partial(jnp.dot, preferred_element_type=F32)
    return dot(high, matrix_ref[0]) + dot(low, matrix_ref[0]) + dot(high, matrix_ref[1])


def blurred_chunk(along_z, first, left, right):
    rows = [left_product(left[...], along_z[first + k]) for k in range(CHUNK)]
    return right_product(jnp.concatenate(rows, axis=0), right)


def back_chunk(ratio, first, left, right, out_ref):
    rows = out_ref.shape[1] - 2 * EDGE
    across = right_product(ratio, right)
    for k in range(CHUNK):
        out_ref[first + k] = left_product(left[...], across[k * rows : (k + 1) * rows])


def z_back(tap_lists, sources, segments):
    depth, _, width = sources[0].shape

    for first, count, store in segments:

        def strip(step, carry, first=first, store=store):
            row = pl.multiple_of(step * EDGE, EDGE)
            for lane in range(0, width, 128):
                lanes = pl.ds(lane, 128)
                window = pl.ds(row + first * EDGE, EDGE)
                plane_lists = [[ref[z, window, lanes] for z in range(depth)] for ref in sources]
                for o, total in enumerate(scatter_planes(tap_lists, plane_lists)):
                    store(o, row, lanes, total)
            return carry

        lax.fori_loop(0, count, strip, 0)


def read_taps(ref, view, flip):
    taps = [ref[view, 0, t] for t in range(ref.shape[2])]
    total = jnp.full((EDGE, 128), sum(taps), F32)
    taps = [jnp.full((EDGE, 128), tap, F32) / total for tap in taps]
    return taps[::-1] if flip else taps


def blur_into(out_ref, taps, extended, along_z, left, right):
    depth, rows, _ = out_ref.shape
    z_forward(taps, extended, along_z)
    for first in range(0, depth, CHUNK):
        blurred = blurred_chunk(along_z, first, left, right)
        for k in range(CHUNK):
            out_ref[first + k] = blurred[k * rows : (k + 1) * rows]


def ratios_back(seen_planes, blurred, left, right, back):
    for first in range(0, blurred.shape[0], CHUNK):
        ratio = jnp.concatenate(
            [seen_planes[first + k] / blurred[first + k] for k in range(CHUNK)], axis=0
        )
        back_chunk(ratio, first, left, right, back)


class Mirrored:
    def __init__(self, low_half, high_half):
        planes = [(ref, z) for ref in (low_half, high_half) for z in range(ref.shape[0])]
        self.planes = planes[::-1]

    def __getitem__(self, index):
        ref, z = self.planes[index]
        return ref[z]


def forward_kernel(taps_ref, *refs):
    center, z_low, z_high, y_low, y_high = refs[:5]
    mats = refs[5:9]
    extended, blurred, along_z = refs[9], refs[10:12], refs[12]
    depth, rows, _ = center.shape
    reach = z_low.shape[0]
    inner = pl.ds(EDGE, rows)
    extended[:reach, inner] = z_low[...]
    extended[pl.ds(reach, depth), inner] = center[...]
    extended[pl.ds(reach + depth, reach), inner] = z_high[...]
    extended[:, :EDGE] = y_low[...]
    extended[:, pl.ds(EDGE + rows, EDGE)] = y_high[...]
    for v in range(2):
        taps = read_taps(taps_ref, v, v == 1)
        blur_into(blurred[v], taps, extended, along_z, mats[2 * v], mats[2 * v + 1])


def back_kernel(taps_ref, *refs):
    blurred, view_one, halves, mats = refs[:2], refs[2], refs[3:5], refs[5:9]
    y_low, y_mid, y_high = refs[9:12]
    backs = refs[12:14]
    ratios_back(view_one, blurred[0], mats[0], mats[1], backs[0])
    ratios_back(Mirrored(*halves), blurred[1], mats[2], mats[3], backs[1])
    segments = []
    first = 0
    for ref in (y_low, y_mid, y_high):

        def store(o, row, lanes, total, ref=ref):
            ref[o, pl.ds(row, EDGE), lanes] = total

        segments.append((first, ref.shape[1] // EDGE, store))
        first += ref.shape[1] // EDGE
    z_back([read_taps(taps_ref, 0, False), read_taps(taps_ref, 1, True)], backs, segments)


def parity(axis):
    return lax.rem(lax.axis_index(axis), 2)


def by_core(low_and_high):
    core = parity("xy")

    @pl.when(core == 0)
    def _():
        low_and_high(1, 0)

    @pl.when(core == 1)
    def _():
        low_and_high(0, 1)


def row_sum_kernel(y_low, y_mid, y_high, from_below, from_above, near, z_mid, far):
    edge, inner = y_low.shape[1], y_mid.shape[1]

    def fill(low, high):
        sides = (near, far)
        first = 0
        for ref in (sides[low], z_mid, sides[high]):
            planes = pl.ds(first, ref.shape[0])
            ref[:, :edge] = y_low[planes] + from_below[planes]
            ref[:, pl.ds(edge, inner)] = y_mid[planes]
            ref[:, pl.ds(edge + inner, edge)] = y_high[planes] + from_above[planes]
            first += ref.shape[0]

    by_core(fill)


def second_kernel(taps_ref, *refs):
    before, near, z_mid, far, from_near, from_far = refs[:6]
    view_one, halves, mats = refs[6], refs[7:9], refs[9:17]
    y_low_out, y_high_out, z_low_out, z_mid_out, z_high_out = refs[17:22]
    estimate, along_z, backs = refs[22], refs[23], refs[24:26]
    overlap, middle = near.shape[0], z_mid.shape[0]

    def fill(low, high):
        sides = ((near, from_near), (far, from_far))
        for (mine, other), first in ((sides[low], 0), (sides[high], overlap + middle)):
            for o in range(overlap):
                estimate[first + o] = before[first + o] * (mine[o] + other[o]) * 0.5

    by_core(fill)
    for o in range(middle):
        estimate[overlap + o] = before[overlap + o] * z_mid[o] * 0.5
    taps = [read_taps(taps_ref, 0, False), read_taps(taps_ref, 1, True)]
    seen = (view_one, Mirrored(*halves))
    for v in range(2):
        left, back_left, right, back_right = mats[4 * v : 4 * v + 4]
        z_forward(taps[v], estimate, along_z)
        for first in range(0, view_one.shape[0], CHUNK):
            blurred = blurred_chunk(along_z, first, left, right)
            ratio = jnp.concatenate([seen[v][first + k] for k in range(CHUNK)], axis=0) / blurred
            back_chunk(ratio, first, back_left, back_right, backs[v])
    rows = z_mid_out.shape[1]
    reach = z_low_out.shape[0]
    depth = z_mid_out.shape[0]

    def scaled(o, row, lanes, total):
        return total * estimate[o, pl.ds(row, EDGE), lanes] * 0.5

    def store_low(o, row, lanes, total):
        y_low_out[o, :, lanes] = scaled(o, 0, lanes, total)

    def store_high(o, row, lanes, total):
        y_high_out[o, :, lanes] = scaled(o, rows + EDGE, lanes, total)

    def store_inner(o, row, lanes, total):
        value = scaled(o, pl.multiple_of(row + EDGE, EDGE), lanes, total)
        if o < reach:
            ref, plane = z_low_out, o
        elif o < reach + depth:
            ref, plane = z_mid_out, o - reach
        else:
            ref, plane = z_high_out, o - reach - depth
        ref[plane, pl.ds(row, EDGE), lanes] = value

    strips = rows // EDGE
    z_back(
        taps, backs, [(0, 1, store_low), (1, strips, store_inner), (strips + 1, 1, store_high)]
    )


def last_row_sum_kernel(
    z_low, z_mid, z_high, from_below, from_above, near, far, ready, late
):
    rows = z_mid.shape[1]
    reach, half = near.shape[0], ready.shape[0]

    def put(out, ref, start, first):
        source = pl.ds(start, out.shape[0])
        planes = pl.ds(first + start, out.shape[0])
        out[:, :EDGE] = ref[source, :EDGE] + from_below[planes]
        inner = pl.ds(EDGE, rows - 2 * EDGE)
        out[:, inner] = ref[source, inner]
        tail = pl.ds(rows - EDGE, EDGE)
        out[:, tail] = ref[source, tail] + from_above[planes]

    def fill(low, high):
        put((near, far)[low], z_low, 0, 0)
        put((ready, late)[low], z_mid, 0, reach)
        put((ready, late)[high], z_mid, half, reach)
        put((near, far)[high], z_high, 0, reach + z_mid.shape[0])

    by_core(fill)


def add_planes_kernel(late, planes, other, out):
    core = parity("xy")
    out[...] = planes[...]
    window = pl.ds(core if late else 1 - core, other.shape[0])
    out[window] = out[window] + other[...]


def join_kernel(ready, late, out):
    half = ready.shape[0]
    slab = parity("gz")
    out[pl.ds((1 - slab) * half, half)] = ready[...]
    out[pl.ds(slab * half, half)] = late[...]


def edge_kernel(center, z_low, z_high, low_rows, high_rows):
    rows = center.shape[1]
    first = 0
    for ref in (z_low, center, z_high):
        planes = pl.ds(first, ref.shape[0])
        low_rows[planes] = ref[:, :EDGE]
        high_rows[planes] = ref[:, pl.ds(rows - EDGE, EDGE)]
        first += ref.shape[0]


def call(kernel, arrays, outs, scratch=(), scalars=1):
    vmem = pl.BlockSpec(memory_space=pltpu.VMEM)
    smem = pl.BlockSpec(memory_space=pltpu.SMEM)
    return pl.pallas_call(
        kernel,
        out_shape=[jax.ShapeDtypeStruct(shape, F32) for shape in outs],
        in_specs=[smem] * scalars + [vmem] * (len(arrays) - scalars),
        out_specs=[vmem] * len(outs),
        scratch_shapes=[pltpu.VMEM(shape, F32) for shape in scratch],
        compiler_params=pltpu.CompilerParams(vmem_limit_bytes=LIMIT),
    )(*arrays)


def local(view_one, view_two, estimate, psf):
    depth, rows, width = estimate.shape
    reach = psf.shape[2] // 2
    one, two = filter_matrices(psf, rows, width)
    full = depth + 2 * reach

    def same(slab, tile):
        return slab, tile

    def across(slab, tile):
        return SLABS - 1 - slab, tile

    half = depth * PART // 16
    first_half = moved(view_two[:half], given, working, across)
    z_low = moved(estimate[depth - reach :], given, working, lambda s, t: (s + 1, t))
    z_high = moved(estimate[:reach], given, working, lambda s, t: (s - 1, t))
    second_half = moved(view_two[half:], given, working, across)
    estimate = moved(estimate, given, working, same)

    low_rows, high_rows = call(
        edge_kernel,
        (estimate, z_low, z_high),
        [(full, EDGE, width)] * 2,
        scalars=0,
    )
    y_low = along_tiles(high_rows, 1)
    y_high = along_tiles(low_rows, -1)
    view_one = moved(view_one, given, working, same)

    tall = (depth, rows + 2 * EDGE, width)
    extended = (full, rows + 2 * EDGE, width)
    before, *blurred = call(
        forward_kernel,
        (psf, estimate, z_low, z_high, y_low, y_high, one[0], one[2], two[0], two[2]),
        [extended, view_one.shape, view_one.shape],
        [tall],
    )
    y_low, y_mid, y_high = call(
        back_kernel,
        (psf, *blurred, view_one, first_half, second_half, one[1], one[3], two[1], two[3]),
        [(full, 2 * EDGE, width), (full, rows - 2 * EDGE, width), (full, 2 * EDGE, width)],
        [tall, tall],
    )
    from_below = along_tiles(y_high, 1)
    from_above = along_tiles(y_low, -1)
    overlap = 2 * reach
    near, z_mid, far = call(
        row_sum_kernel,
        (y_low, y_mid, y_high, from_below, from_above),
        [(n, rows + 2 * EDGE, width) for n in (overlap, full - 2 * overlap, overlap)],
        scalars=0,
    )
    from_far = to_other_chip(far)
    from_near = to_other_core(near)
    y_low, y_high, *pieces = call(
        second_kernel,
        (psf, before, near, z_mid, far, from_near, from_far)
        + (view_one, first_half, second_half, *one, *two),
        [(full, EDGE, width)] * 2 + [(n, rows, width) for n in (reach, depth, reach)],
        [extended, tall, tall, tall],
    )
    from_below = along_tiles(y_high, 1)
    from_above = along_tiles(y_low, -1)
    near, far, ready, late = call(
        last_row_sum_kernel,
        (*pieces, from_below, from_above),
        [(n, rows, width) for n in (reach, reach, depth // 2, depth // 2)],
        scalars=0,
    )
    from_near = to_other_core(near)
    from_far = to_other_chip(far)
    (ready,) = call(
        functools.partial(add_planes_kernel, False),
        (ready, from_near),
        [ready.shape],
        scalars=0,
    )
    ready = moved(ready, working, given, same)
    (late,) = call(
        functools.partial(add_planes_kernel, True), (late, from_far), [late.shape], scalars=0
    )
    late = moved(late, working, given, same)
    (result,) = call(join_kernel, (ready, late), [(depth, rows, width)], scalars=0)
    return result


def solution(mesh):
    return jax.shard_map(
        local,
        mesh=mesh,
        in_specs=(P("gz", "xy", None), P("gz", "xy", None), P("gz", "xy", None), P()),
        out_specs=P("gz", "xy", None),
        check_vma=False,
    )
```
